256 devices in a mesh: dp: 16 (over y_hi, x, core), seq: 16 (over z, y_lo).
Axes of the slice: x: 4, y: 4 (y_hi: 2, y_lo: 2; y = y_hi * 2 + y_lo), z: 8, core: 2. Of those that a mesh axis runs over, the one named last changes fastest.
Arguments:
- query_rows: bfloat16 [32768, 4096], P(('dp', 'seq')), parts along dimension 0, may hold values from -32 to 32
- key_rows: bfloat16 [32768, 4096], P(('dp', 'seq')), parts along dimension 0, may hold values from -32 to 32
- value_rows: bfloat16 [32768, 4096], P(('dp', 'seq')), parts along dimension 0, may hold values from -6 to 6
- query_tangent: bfloat16 [32768, 4096], P(('dp', 'seq')), parts along dimension 0, may hold values from -6 to 6
- key_tangent: bfloat16 [32768, 4096], P(('dp', 'seq')), parts along dimension 0, may hold values from -6 to 6
- value_tangent: bfloat16 [32768, 4096], P(('dp', 'seq')), parts along dimension 0, may hold values from -6 to 6
Outputs:
- attended: bfloat16 [32768, 4096], P(('dp', 'seq')), parts along dimension 0
- attended_tangent: bfloat16 [32768, 4096], P(('dp', 'seq')), parts along dimension 0
The draws below stay inside these ranges and needn't reach their ends.
There are 16 independent parts, one for each index of `dp`. The reference program is written for one: setup_inputs(seed, part) draws one part's arguments, and reference() takes and returns one part's arrays. A program takes and returns all parts, laid end to end along the dimension named above; each array names one. Nothing has to cross between parts.
All inputs are finite; a program needn't handle non-finite values.
Results may differ from the reference program's by a relative error of at most 0.0049.
Values may be sent and summed in bfloat16 or wider, within the bound.
A program may use at most 64 MiB of HBM per device.

```python
import jax
import jax.numpy as jnp
from jax import lax

HEADS = 32
HEAD = 128
TOKENS = 2048


def draw_query_rows(key, part):
    fresh_key = jax.random.fold_in(key, 11)
    sample = jnp.clip(1.4 * jax.random.normal(fresh_key, (TOKENS, HEADS, HEAD), jnp.float32), -8.0, 8.0)
    return sample.reshape(TOKENS, HEADS * HEAD).astype(jnp.bfloat16)


def draw_key_rows(key, part):
    fresh_key = jax.random.fold_in(key, 13)
    sample = jnp.clip(1.4 * jax.random.normal(fresh_key, (TOKENS, HEADS, HEAD), jnp.float32), -8.0, 8.0)
    return sample.reshape(TOKENS, HEADS * HEAD).astype(jnp.bfloat16)


def level_of(rng, shape, cuts, low, top_value):
    def one(position, parts):
        steps = jax.random.uniform(jax.random.fold_in(jax.random.fold_in(rng, 6), position), (parts,), jnp.float32, low / len(cuts), top_value / len(cuts))
        return jnp.repeat(jnp.exp(steps), shape[position] // parts).reshape((-1,) + (1,) * (len(shape) - position - 1))

    loudness = one(*cuts[0])
    for cut in cuts[1:]:
        loudness = loudness * one(*cut)
    return loudness


def bell_draw(rng, shape, width, most, cuts=(), kind=jnp.bfloat16):
    level = level_of(rng, shape, cuts, -0.22, 0.18) if cuts else 1.0
    array = jax.random.normal(rng, shape, jnp.float32) * width * level
    return jnp.minimum(jnp.maximum(array, -most), most).astype(kind)


def setup_inputs(seed: int = 0, part: int = 0) -> dict:
    streams_of = jax.random.split(jax.random.key(seed), 7)
    part_keys = jax.random.split(jax.random.fold_in(streams_of[6], part), 7)
    return {
        "query_rows": draw_query_rows(jax.random.fold_in(jax.random.fold_in(streams_of[6], part), 71), part),
        "key_rows": draw_key_rows(jax.random.fold_in(jax.random.fold_in(streams_of[6], part), 71), part),
        "value_rows": bell_draw(part_keys[2], (TOKENS, HEADS * HEAD), 1.0, 6.0, ((0, 16),)),
        "query_tangent": bell_draw(part_keys[3], (TOKENS, HEADS * HEAD), 1.0, 6.0, ((0, 16),)),
        "key_tangent": bell_draw(part_keys[4], (TOKENS, HEADS * HEAD), 1.0, 6.0, ((0, 16),)),
        "value_tangent": bell_draw(part_keys[5], (TOKENS, HEADS * HEAD), 1.0, 6.0, ((0, 16),)),
    }


def one_head(pieces):
    head_queries, head_keys, head_values, query_tangent, key_tangent, value_tangent = pieces
    score_scale = HEAD ** -0.5
    scores = jnp.dot(head_queries, head_keys.T, preferred_element_type=jnp.float32) * score_scale
    score_tangent = (jnp.dot(query_tangent, head_keys.T, preferred_element_type=jnp.float32)
                     + jnp.dot(head_queries, key_tangent.T, preferred_element_type=jnp.float32)) * score_scale
    row_max = jnp.max(scores, axis=1, keepdims=True)
    raised = jnp.exp(scores - row_max)
    exact_weights = raised / jnp.sum(raised, axis=1, keepdims=True)
    weights = exact_weights.astype(jnp.bfloat16)
    output = jnp.dot(weights, head_values, preferred_element_type=jnp.float32).astype(jnp.bfloat16)
    mean_tangent = jnp.sum(exact_weights * score_tangent, axis=1, keepdims=True)
    weight_tangent = (exact_weights * (score_tangent - mean_tangent)).astype(jnp.bfloat16)
    tangent = (jnp.dot(weight_tangent, head_values, preferred_element_type=jnp.float32)
               + jnp.dot(weights, value_tangent, preferred_element_type=jnp.float32)).astype(jnp.bfloat16)
    return output, tangent


def by_heads(matrix):
    return matrix.reshape(TOKENS, HEADS, HEAD).transpose(1, 0, 2)


def reference(query_rows, key_rows, value_rows, query_tangent, key_tangent, value_tangent):
    outputs, tangents = lax.map(one_head, (by_heads(query_rows), by_heads(key_rows), by_heads(value_rows),
                                           by_heads(query_tangent), by_heads(key_tangent), by_heads(value_tangent)))
    attended = outputs.transpose(1, 0, 2).reshape(TOKENS, HEADS * HEAD)
    attended_tangent = tangents.transpose(1, 0, 2).reshape(TOKENS, HEADS * HEAD)
    return attended, attended_tangent
```

```python
import functools
import math

import jax
import jax.numpy as jnp
from jax import lax
from jax.experimental import pallas as pl
from jax.experimental.pallas import tpu as pltpu
from jax.sharding import PartitionSpec as P

HEADS = 32
HEAD = 128
MESH_ID = pl.DeviceIdType.MESH
NT = (((1,), (1,)), ((), ()))
NN = (((1,), (0,)), ((), ()))


def kernel(
    groups,
    q_ref,
    k_ref,
    v_ref,
    dq_ref,
    dk_ref,
    dv_ref,
    out_ref,
    dout_ref,
    held,
    result,
    in_send,
    in_recv,
    out_send,
    out_recv,
):
    me = lax.axis_index("seq")
    rows = q_ref.shape[0]
    per_group = HEADS // groups
    steps = groups // 2
    pair = 2 * rows
    scale = HEAD ** (-0.5)
    my_z, my_y = me // 2, me % 2

    def far_first(i):
        distance = (steps - i) // 2
        sign = 2 * (i % 2) - 1
        return lax.rem(my_z + sign * distance + steps, steps)

    barrier = pltpu.get_barrier_semaphore()

    def greet(j, carry):
        pl.semaphore_signal(
            barrier, inc=1, device_id={"seq": lax.rem(me + j, groups)}, device_id_type=MESH_ID
        )
        return carry

    lax.fori_loop(1, groups, greet, 0)

    plan = ((k_ref, 1, 0), (dk_ref, 1, HEAD), (dq_ref, 0, 0), (q_ref, 0, HEAD), (v_ref, 2, 0), (dv_ref, 2, HEAD))

    def piece(source, kind, column, h, peer):
        src = source.at[:, pl.ds(pl.multiple_of((peer * per_group + h) * HEAD, HEAD), HEAD)]
        dst = held.at[h, kind, pl.ds(pl.multiple_of(me * rows, rows), rows), pl.ds(column, HEAD)]
        return src, dst

    for h in range(per_group):
        for source, kind, column in plan:
            src, dst = piece(source, kind, column, h, me)
            pltpu.make_async_copy(src, dst, in_recv.at[h]).start()

    pl.semaphore_wait(barrier, groups - 1)

    for h in range(per_group):

        def send_to(j, carry, h=h):
            peer = far_first(j // 2) * 2 + lax.rem(my_y + j + 1, 2)
            for source, kind, column in plan:
                src, dst = piece(source, kind, column, h, peer)
                pltpu.make_async_remote_copy(
                    src_ref=src,
                    dst_ref=dst,
                    send_sem=in_send,
                    recv_sem=in_recv.at[h],
                    device_id={"seq": peer},
                    device_id_type=MESH_ID,
                ).start()
            return carry

        lax.fori_loop(0, groups - 1, send_to, 0)

    def give(g, target_y, own):
        h, z = g // steps, far_first(g % steps)
        target = z * 2 + target_y
        for part, ref in ((0, out_ref), (1, dout_ref)):
            src = result.at[h, pl.ds(pl.multiple_of(target * rows, rows), rows), pl.ds(part * HEAD, HEAD)]
            dst = ref.at[:, pl.ds(pl.multiple_of((me * per_group + h) * HEAD, HEAD), HEAD)]
            if own:
                pltpu.make_async_copy(src, dst, out_recv.at[part]).start()
            else:
                pltpu.make_async_remote_copy(
                    src_ref=src,
                    dst_ref=dst,
                    send_sem=out_send,
                    recv_sem=out_recv.at[part],
                    device_id={"seq": target},
                    device_id_type=MESH_ID,
                ).start()

    def give_block(g):
        give(g, 1 - my_y, False)

        @pl.when(g % steps == steps - 1)
        def _():
            give(g, my_y, True)

        @pl.when(g % steps != steps - 1)
        def _():
            give(g, my_y, False)

    def block(g, carry):
        h = g // steps

        @pl.when(g % steps == 0)
        def _():
            pltpu.make_async_copy(held.at[h], held.at[h], in_recv.at[h]).wait()

        @pl.when(g > 0)
        def _():
            give_block(g - 1)

        where = pl.ds(pl.multiple_of(far_first(g % steps) * pair, pair), pair)
        both = held[h, 0, where, :]
        keys = held[h, 1]
        values = held[h, 2]
        scores = lax.dot_general(both[:, HEAD:], keys[:, :HEAD], NT, preferred_element_type=jnp.float32)
        tangent = lax.dot_general(both, keys, NT, preferred_element_type=jnp.float32)
        row_max = jnp.max(scores, axis=1, keepdims=True)
        raised = jnp.exp2((scores - row_max) * (scale * math.log2(math.e)))
        inverse = 1.0 / jnp.sum(raised, axis=1, keepdims=True)
        exact = raised * inverse
        mean = jnp.sum(exact * tangent, axis=1, keepdims=True)
        weights = exact.astype(jnp.bfloat16)
        turned = (exact * (tangent - mean)).astype(jnp.bfloat16)
        plain = lax.dot_general(weights, values, NN, preferred_element_type=jnp.float32)
        moved = lax.dot_general(turned, values[:, :HEAD], NN, preferred_element_type=jnp.float32)
        result[h, where, :HEAD] = plain[:, :HEAD].astype(jnp.bfloat16)
        result[h, where, HEAD:] = (moved * scale + plain[:, HEAD:]).astype(jnp.bfloat16)
        return carry

    last = per_group * steps - 1
    lax.fori_loop(0, last + 1, block, 0)
    sent = held.at[:, :, pl.ds(0, (groups - 1) * rows), :]
    pltpu.make_async_copy(sent, sent, in_send).wait()
    give_block(last)
    given = result.at[:, pl.ds(0, (groups - 1) * rows), :]
    pltpu.make_async_copy(given, given, out_send).wait()
    pltpu.make_async_copy(out_ref, out_ref, out_recv.at[0]).wait()
    pltpu.make_async_copy(dout_ref, dout_ref, out_recv.at[1]).wait()


def on_device(*args):
    groups = lax.axis_size("seq")
    per_group = HEADS // groups
    tokens = args[0].shape[0] * groups
    shape = jax.ShapeDtypeStruct(args[0].shape, jnp.bfloat16)
    return pl.pallas_call(
        functools.partial(kernel, groups),
        out_shape=(shape, shape),
        in_specs=[pl.BlockSpec(memory_space=pl.ANY)] * 6,
        out_specs=(pl.BlockSpec(memory_space=pl.ANY),) * 2,
        scratch_shapes=[
            pltpu.VMEM((per_group, 3, tokens, 2 * HEAD), jnp.bfloat16),
            pltpu.VMEM((per_group, tokens, 2 * HEAD), jnp.bfloat16),
            pltpu.SemaphoreType.DMA,
            pltpu.SemaphoreType.DMA((per_group,)),
            pltpu.SemaphoreType.DMA,
            pltpu.SemaphoreType.DMA((2,)),
        ],
        compiler_params=pltpu.CompilerParams(collective_id=0, has_side_effects=True),
        name="attention_tangent",
    )(*args)


def solution(mesh):
    spec = P(("dp", "seq"), None)
    return jax.shard_map(
        on_device, mesh=mesh, in_specs=(spec,) * 6, out_specs=(spec, spec), check_vma=False
    )
```

```python
import functools
import math

import jax
import jax.numpy as jnp
from jax import lax
from jax.experimental import pallas as pl
from jax.experimental.pallas import tpu as pltpu
from jax.sharding import PartitionSpec as P

HEADS = 32
HEAD = 128
MESH_ID = pl.DeviceIdType.MESH
NT = (((1,), (1,)), ((), ()))
NN = (((1,), (0,)), ((), ()))


def kernel(
    groups,
    q_ref,
    k_ref,
    v_ref,
    dq_ref,
    dk_ref,
    dv_ref,
    out_ref,
    dout_ref,
    held,
    result,
    in_send,
    in_recv,
    out_send,
    out_recv,
    rounds,
):
    me = lax.axis_index("seq")
    rows = q_ref.shape[0]
    per_group = HEADS // groups
    steps = groups // 2
    pair = 2 * rows
    scale = HEAD ** (-0.5)
    my_z, my_y = me // 2, me % 2

    def far_first(i):
        distance = (steps - i) // 2
        sign = 2 * (i % 2) - 1
        return lax.rem(my_z + sign * distance + steps, steps)

    def at(distance, y):
        return lax.rem(my_z + distance + steps, steps) * 2 + y

    neighbours = (at(1, my_y), at(-1, my_y))
    barrier = pltpu.get_barrier_semaphore()
    for peer in neighbours + (at(0, 1 - my_y),):
        pl.semaphore_signal(barrier, inc=1, device_id={"seq": peer}, device_id_type=MESH_ID)

    plan = ((k_ref, 1, 0), (dk_ref, 1, HEAD), (dq_ref, 0, 0), (q_ref, 0, HEAD), (v_ref, 2, 0), (dv_ref, 2, HEAD))

    def piece(source, kind, column, h, peer):
        src = source.at[:, pl.ds(pl.multiple_of((peer * per_group + h) * HEAD, HEAD), HEAD)]
        dst = held.at[h, kind, pl.ds(pl.multiple_of(me * rows, rows), rows), pl.ds(column, HEAD)]
        return src, dst

    for h in range(per_group):
        for source, kind, column in plan:
            src, dst = piece(source, kind, column, h, me)
            pltpu.make_async_copy(src, dst, in_recv.at[h]).start()

    def send_to(h, peer):
        for source, kind, column in plan:
            src, dst = piece(source, kind, column, h, peer)
            pltpu.make_async_remote_copy(
                src_ref=src,
                dst_ref=dst,
                send_sem=in_send,
                recv_sem=in_recv.at[h],
                device_id={"seq": peer},
                device_id_type=MESH_ID,
            ).start()

    pl.semaphore_wait(barrier, 3)
    half = steps // 2
    for hops in range(1, half + 2):
        if hops > 1:
            for peer in neighbours:
                pl.semaphore_signal(
                    rounds.at[hops - 2], inc=1, device_id={"seq": peer}, device_id_type=MESH_ID
                )
            pl.semaphore_wait(rounds.at[hops - 2], 2)
        for distance, y in ((hops - 1, 1 - my_y), (hops, my_y)):
            if distance <= half:
                for sign in (1, -1) if 0 < distance < half else (1,):
                    send_to(0, at(sign * distance, y))

    for h in range(1, per_group):

        def send_rest(j, carry, h=h):
            i = groups - 2 - j
            peer = far_first(i // 2) * 2 + lax.rem(my_y + i + 1, 2)
            send_to(h, peer)
            return carry

        lax.fori_loop(0, groups - 1, send_rest, 0)

    def give(g, target_y, own):
        h, z = g // steps, far_first(g % steps)
        target = z * 2 + target_y
        for part, ref in ((0, out_ref), (1, dout_ref)):
            src = result.at[h, pl.ds(pl.multiple_of(target * rows, rows), rows), pl.ds(part * HEAD, HEAD)]
            dst = ref.at[:, pl.ds(pl.multiple_of((me * per_group + h) * HEAD, HEAD), HEAD)]
            if own:
                pltpu.make_async_copy(src, dst, out_recv.at[part]).start()
            else:
                pltpu.make_async_remote_copy(
                    src_ref=src,
                    dst_ref=dst,
                    send_sem=out_send,
                    recv_sem=out_recv.at[part],
                    device_id={"seq": target},
                    device_id_type=MESH_ID,
                ).start()

    def give_block(g):
        give(g, 1 - my_y, False)

        @pl.when(g % steps == steps - 1)
        def _():
            give(g, my_y, True)

        @pl.when(g % steps != steps - 1)
        def _():
            give(g, my_y, False)

    def block(g, carry):
        h = g // steps

        @pl.when(g % steps == 0)
        def _():
            pltpu.make_async_copy(held.at[h], held.at[h], in_recv.at[h]).wait()

        @pl.when(g > 0)
        def _():
            give_block(g - 1)

        where = pl.ds(pl.multiple_of(far_first(g % steps) * pair, pair), pair)
        both = held[h, 0, where, :]
        keys = held[h, 1]
        values = held[h, 2]
        scores = lax.dot_general(both[:, HEAD:], keys[:, :HEAD], NT, preferred_element_type=jnp.float32)
        tangent = lax.dot_general(both, keys, NT, preferred_element_type=jnp.float32)
        row_max = jnp.max(scores, axis=1, keepdims=True)
        raised = jnp.exp2((scores - row_max) * (scale * math.log2(math.e)))
        inverse = 1.0 / jnp.sum(raised, axis=1, keepdims=True)
        exact = raised * inverse
        mean = jnp.sum(exact * tangent, axis=1, keepdims=True)
        weights = exact.astype(jnp.bfloat16)
        turned = (exact * (tangent - mean)).astype(jnp.bfloat16)
        plain = lax.dot_general(weights, values, NN, preferred_element_type=jnp.float32)
        moved = lax.dot_general(turned, values[:, :HEAD], NN, preferred_element_type=jnp.float32)
        result[h, where, :HEAD] = plain[:, :HEAD].astype(jnp.bfloat16)
        result[h, where, HEAD:] = (moved * scale + plain[:, HEAD:]).astype(jnp.bfloat16)
        return carry

    last = per_group * steps - 1
    lax.fori_loop(0, last + 1, block, 0)
    sent = held.at[:, :, pl.ds(0, (groups - 1) * rows), :]
    pltpu.make_async_copy(sent, sent, in_send).wait()
    give_block(last)
    given = result.at[:, pl.ds(0, (groups - 1) * rows), :]
    pltpu.make_async_copy(given, given, out_send).wait()
    pltpu.make_async_copy(out_ref, out_ref, out_recv.at[0]).wait()
    pltpu.make_async_copy(dout_ref, dout_ref, out_recv.at[1]).wait()


def put_out(a_ref, b_ref, a_out, b_out, sems):
    copies = [
        pltpu.make_async_copy(a_ref, a_out, sems.at[0]),
        pltpu.make_async_copy(b_ref, b_out, sems.at[1]),
    ]
    for copy in copies:
        copy.start()
    for copy in copies:
        copy.wait()


def on_device(*args):
    groups = lax.axis_size("seq")
    per_group = HEADS // groups
    tokens = args[0].shape[0] * groups
    shape = jax.ShapeDtypeStruct(args[0].shape, jnp.bfloat16)
    landed = pl.pallas_call(
        functools.partial(kernel, groups),
        out_shape=(pltpu.VMEM(args[0].shape, jnp.bfloat16),) * 2,
        in_specs=[pl.BlockSpec(memory_space=pl.ANY)] * 6,
        out_specs=(pl.BlockSpec(memory_space=pl.ANY),) * 2,
        scratch_shapes=[
            pltpu.VMEM((per_group, 3, tokens, 2 * HEAD), jnp.bfloat16),
            pltpu.VMEM((per_group, tokens, 2 * HEAD), jnp.bfloat16),
            pltpu.SemaphoreType.DMA,
            pltpu.SemaphoreType.DMA((per_group,)),
            pltpu.SemaphoreType.DMA,
            pltpu.SemaphoreType.DMA((2,)),
            pltpu.SemaphoreType.REGULAR((groups // 4,)),
        ],
        compiler_params=pltpu.CompilerParams(collective_id=0, has_side_effects=True),
        name="attention_tangent",
    )(*args)
    return pl.pallas_call(
        put_out,
        out_shape=(shape, shape),
        in_specs=[pl.BlockSpec(memory_space=pl.ANY)] * 2,
        out_specs=(pl.BlockSpec(memory_space=pl.ANY),) * 2,
        scratch_shapes=[pltpu.SemaphoreType.DMA((2,))],
        name="put_out",
    )(*(pltpu.with_memory_space_constraint(x, pltpu.VMEM) for x in landed))


def solution(mesh):
    spec = P(("dp", "seq"), None)
    return jax.shard_map(
        on_device, mesh=mesh, in_specs=(spec,) * 6, out_specs=(spec, spec), check_vma=False
    )
```

```python
import functools

import jax
import jax.numpy as jnp
from jax import lax
from jax.experimental import pallas as pl
from jax.experimental.pallas import tpu as pltpu
from jax.sharding import PartitionSpec as P

HEADS = 32
HEAD = 128
MESH_ID = pl.DeviceIdType.MESH
NT = (((1,), (1,)), ((), ()))
NN = (((1,), (0,)), ((), ()))


def kernel(
    groups,
    q_ref,
    k_ref,
    v_ref,
    dq_ref,
    dk_ref,
    dv_ref,
    out_ref,
    dout_ref,
    held,
    result,
    in_send,
    in_recv,
    out_send,
    out_recv,
    rounds,
):
    me = lax.axis_index("seq")
    rows = q_ref.shape[0]
    per_group = HEADS // groups
    steps = groups // 2
    pair = 2 * rows
    scale = HEAD ** (-0.5)
    my_z, my_y = me // 2, me % 2

    def far_first(i):
        distance = (steps - i) // 2
        sign = 2 * (i % 2) - 1
        return lax.rem(my_z + sign * distance + steps, steps)

    def at(distance, y):
        return lax.rem(my_z + distance + steps, steps) * 2 + y

    neighbours = (at(1, my_y), at(-1, my_y))
    barrier = pltpu.get_barrier_semaphore()
    for peer in neighbours + (at(0, 1 - my_y),):
        pl.semaphore_signal(barrier, inc=1, device_id={"seq": peer}, device_id_type=MESH_ID)

    plan = ((k_ref, 1, 0), (dk_ref, 1, HEAD), (dq_ref, 0, 0), (q_ref, 0, HEAD), (v_ref, 2, 0), (dv_ref, 2, HEAD))

    def piece(source, kind, column, h, peer):
        src = source.at[:, pl.ds(pl.multiple_of((peer * per_group + h) * HEAD, HEAD), HEAD)]
        dst = held.at[h, kind, pl.ds(pl.multiple_of(me * rows, rows), rows), pl.ds(column, HEAD)]
        return src, dst

    for h in range(per_group):
        for source, kind, column in plan:
            src, dst = piece(source, kind, column, h, me)
            pltpu.make_async_copy(src, dst, in_recv.at[h]).start()

    def send_to(h, peer, part=plan):
        for source, kind, column in part:
            src, dst = piece(source, kind, column, h, peer)
            pltpu.make_async_remote_copy(
                src_ref=src,
                dst_ref=dst,
                send_sem=in_send,
                recv_sem=in_recv.at[h],
                device_id={"seq": peer},
                device_id_type=MESH_ID,
            ).start()

    pl.semaphore_wait(barrier, 3)
    half = steps // 2
    for hops in range(1, half + 2):
        if hops > 1:
            for peer in neighbours:
                pl.semaphore_signal(
                    rounds.at[hops - 2], inc=1, device_id={"seq": peer}, device_id_type=MESH_ID
                )
            pl.semaphore_wait(rounds.at[hops - 2], 2)
        for distance, y in ((hops - 1, 1 - my_y), (hops, my_y)):
            if distance <= half:
                for sign in (1, -1) if 0 < distance < half else (1,):
                    send_to(0, at(sign * distance, y))

    for h in range(1, per_group):
        for entry in plan:

            def send_rest(j, carry, h=h, entry=entry):
                i = j
                peer = far_first(i // 2) * 2 + lax.rem(my_y + i + 1, 2)
                send_to(h, peer, (entry,))
                return carry

            lax.fori_loop(0, groups - 1, send_rest, 0)

    def give(g, target_y, own):
        h, z = g // steps, far_first(g % steps)
        target = z * 2 + target_y
        for part, ref in ((0, out_ref), (1, dout_ref)):
            src = result.at[h, pl.ds(pl.multiple_of(target * rows, rows), rows), pl.ds(part * HEAD, HEAD)]
            dst = ref.at[:, pl.ds(pl.multiple_of((me * per_group + h) * HEAD, HEAD), HEAD)]
            if own:
                pltpu.make_async_copy(src, dst, out_recv.at[part]).start()
            else:
                pltpu.make_async_remote_copy(
                    src_ref=src,
                    dst_ref=dst,
                    send_sem=out_send,
                    recv_sem=out_recv.at[part],
                    device_id={"seq": target},
                    device_id_type=MESH_ID,
                ).start()

    def give_block(g):
        give(g, 1 - my_y, False)

        @pl.when(g % steps == steps - 1)
        def _():
            give(g, my_y, True)

        @pl.when(g % steps != steps - 1)
        def _():
            give(g, my_y, False)

    def block(g, carry):
        h = g // steps

        @pl.when(g % steps == 0)
        def _():
            pltpu.make_async_copy(held.at[h], held.at[h], in_recv.at[h]).wait()

        @pl.when(g > 0)
        def _():
            give_block(g - 1)

        where = pl.ds(pl.multiple_of(far_first(g % steps) * pair, pair), pair)
        both = held[h, 0, where, :]
        keys = held[h, 1]
        values = held[h, 2]
        scores = scale * lax.dot_general(
            both[:, HEAD:], keys[:, :HEAD], NT, preferred_element_type=jnp.float32
        )
        tangent = scale * lax.dot_general(both, keys, NT, preferred_element_type=jnp.float32)
        row_max = jnp.max(scores, axis=1, keepdims=True)
        raised = jnp.exp(scores - row_max)
        inverse = 1.0 / jnp.sum(raised, axis=1, keepdims=True)
        exact = raised * inverse
        mean = jnp.sum(exact * tangent, axis=1, keepdims=True)
        weights = exact.astype(jnp.bfloat16)
        turned = (exact * (tangent - mean)).astype(jnp.bfloat16)
        plain = lax.dot_general(weights, values, NN, preferred_element_type=jnp.float32)
        moved = lax.dot_general(turned, values[:, :HEAD], NN, preferred_element_type=jnp.float32)
        result[h, where, :HEAD] = plain[:, :HEAD].astype(jnp.bfloat16)
        result[h, where, HEAD:] = (moved + plain[:, HEAD:]).astype(jnp.bfloat16)
        return carry

    last = per_group * steps - 1
    lax.fori_loop(0, last + 1, block, 0)
    sent = held.at[:, :, pl.ds(0, (groups - 1) * rows), :]
    pltpu.make_async_copy(sent, sent, in_send).wait()
    give_block(last)
    given = result.at[:, pl.ds(0, (groups - 1) * rows), :]
    pltpu.make_async_copy(given, given, out_send).wait()
    pltpu.make_async_copy(out_ref, out_ref, out_recv.at[0]).wait()
    pltpu.make_async_copy(dout_ref, dout_ref, out_recv.at[1]).wait()


def put_out(a_ref, b_ref, a_out, b_out, sems):
    copies = [
        pltpu.make_async_copy(a_ref, a_out, sems.at[0]),
        pltpu.make_async_copy(b_ref, b_out, sems.at[1]),
    ]
    for copy in copies:
        copy.start()
    for copy in copies:
        copy.wait()


def on_device(*args):
    groups = lax.axis_size("seq")
    per_group = HEADS // groups
    tokens = args[0].shape[0] * groups
    shape = jax.ShapeDtypeStruct(args[0].shape, jnp.bfloat16)
    landed = pl.pallas_call(
        functools.partial(kernel, groups),
        out_shape=(pltpu.VMEM(args[0].shape, jnp.bfloat16),) * 2,
        in_specs=[pl.BlockSpec(memory_space=pl.ANY)] * 6,
        out_specs=(pl.BlockSpec(memory_space=pl.ANY),) * 2,
        scratch_shapes=[
            pltpu.VMEM((per_group, 3, tokens, 2 * HEAD), jnp.bfloat16),
            pltpu.VMEM((per_group, tokens, 2 * HEAD), jnp.bfloat16),
            pltpu.SemaphoreType.DMA,
            pltpu.SemaphoreType.DMA((per_group,)),
            pltpu.SemaphoreType.DMA,
            pltpu.SemaphoreType.DMA((2,)),
            pltpu.SemaphoreType.REGULAR((groups // 4,)),
        ],
        compiler_params=pltpu.CompilerParams(collective_id=0, has_side_effects=True),
        name="attention_tangent",
    )(*args)
    return pl.pallas_call(
        put_out,
        out_shape=(shape, shape),
        in_specs=[pl.BlockSpec(memory_space=pl.ANY)] * 2,
        out_specs=(pl.BlockSpec(memory_space=pl.ANY),) * 2,
        scratch_shapes=[pltpu.SemaphoreType.DMA((2,))],
        name="put_out",
    )(*(pltpu.with_memory_space_constraint(x, pltpu.VMEM) for x in landed))


def solution(mesh):
    spec = P(("dp", "seq"), None)
    return jax.shard_map(
        on_device, mesh=mesh, in_specs=(spec,) * 6, out_specs=(spec, spec), check_vma=False
    )
```

```python
import functools

import jax
import jax.numpy as jnp
from jax import lax
from jax.experimental import pallas as pl
from jax.experimental.pallas import tpu as pltpu
from jax.sharding import PartitionSpec as P

HEADS = 32
HEAD = 128
MESH_ID = pl.DeviceIdType.MESH
NT = (((1,), (1,)), ((), ()))
NN = (((1,), (0,)), ((), ()))


def kernel(
    groups,
    q_ref,
    k_ref,
    v_ref,
    dq_ref,
    dk_ref,
    dv_ref,
    out_ref,
    dout_ref,
    held,
    result,
    in_send,
    in_recv,
    out_send,
    out_recv,
    rounds,
):
    me = lax.axis_index("seq")
    rows = q_ref.shape[0]
    per_group = HEADS // groups
    steps = groups // 2
    pair = 2 * rows
    scale = HEAD ** (-0.5)
    my_z, my_y = me // 2, me % 2

    def far_first(i):
        distance = (steps - i) // 2
        sign = 2 * (i % 2) - 1
        return lax.rem(my_z + sign * distance + steps, steps)

    def at(distance, y):
        return lax.rem(my_z + distance + steps, steps) * 2 + y

    neighbours = (at(1, my_y), at(-1, my_y))
    barrier = pltpu.get_barrier_semaphore()
    for peer in neighbours + (at(0, 1 - my_y),):
        pl.semaphore_signal(barrier, inc=1, device_id={"seq": peer}, device_id_type=MESH_ID)

    plan = ((k_ref, 1, 0), (dk_ref, 1, HEAD), (dq_ref, 0, 0), (q_ref, 0, HEAD), (v_ref, 2, 0), (dv_ref, 2, HEAD))

    def piece(source, kind, column, h, peer):
        src = source.at[:, pl.ds(pl.multiple_of((peer * per_group + h) * HEAD, HEAD), HEAD)]
        dst = held.at[h, kind, pl.ds(pl.multiple_of(me * rows, rows), rows), pl.ds(column, HEAD)]
        return src, dst

    for h in range(per_group):
        for source, kind, column in plan:
            src, dst = piece(source, kind, column, h, me)
            pltpu.make_async_copy(src, dst, in_recv.at[h]).start()

    def send_to(h, peer, part=plan):
        for source, kind, column in part:
            src, dst = piece(source, kind, column, h, peer)
            pltpu.make_async_remote_copy(
                src_ref=src,
                dst_ref=dst,
                send_sem=in_send,
                recv_sem=in_recv.at[h],
                device_id={"seq": peer},
                device_id_type=MESH_ID,
            ).start()

    pl.semaphore_wait(barrier, 3)
    half = steps // 2
    for hops in range(1, half + 2):
        if hops > 1:
            for peer in neighbours:
                pl.semaphore_signal(
                    rounds.at[hops - 2], inc=1, device_id={"seq": peer}, device_id_type=MESH_ID
                )
            pl.semaphore_wait(rounds.at[hops - 2], 2)
        for distance, y in ((hops - 1, 1 - my_y), (hops, my_y)):
            if distance <= half:
                for sign in (1, -1) if 0 < distance < half else (1,):
                    send_to(0, at(sign * distance, y))

    for h in range(1, per_group):
        for entry in plan:

            def send_rest(j, carry, h=h, entry=entry):
                peer = far_first(j // 2) * 2 + lax.rem(my_y + j + 1, 2)
                send_to(h, peer, (entry,))
                return carry

            lax.fori_loop(0, groups - 1, send_rest, 0)

    def give(g, target_y, own):
        h, z = g // steps, far_first(g % steps)
        target = z * 2 + target_y
        for part, ref in ((0, out_ref), (1, dout_ref)):
            src = result.at[h, pl.ds(pl.multiple_of(target * rows, rows), rows), pl.ds(part * HEAD, HEAD)]
            dst = ref.at[:, pl.ds(pl.multiple_of((me * per_group + h) * HEAD, HEAD), HEAD)]
            if own:
                pltpu.make_async_copy(src, dst, out_recv.at[part]).start()
            else:
                pltpu.make_async_remote_copy(
                    src_ref=src,
                    dst_ref=dst,
                    send_sem=out_send,
                    recv_sem=out_recv.at[part],
                    device_id={"seq": target},
                    device_id_type=MESH_ID,
                ).start()

    def give_block(g):
        give(g, 1 - my_y, False)

        @pl.when(g % steps == steps - 1)
        def _():
            give(g, my_y, True)

        @pl.when(g % steps != steps - 1)
        def _():
            give(g, my_y, False)

    kept = steps - 3

    def block(g, carry):
        h = g // steps

        @pl.when(g % steps == 0)
        def _():
            pltpu.make_async_copy(held.at[h], held.at[h], in_recv.at[h]).wait()

        where = pl.ds(pl.multiple_of(far_first(g % steps) * pair, pair), pair)
        both = held[h, 0, where, :]
        keys = held[h, 1]
        values = held[h, 2]
        scores = scale * lax.dot_general(
            both[:, HEAD:], keys[:, :HEAD], NT, preferred_element_type=jnp.float32
        )
        tangent = scale * lax.dot_general(both, keys, NT, preferred_element_type=jnp.float32)
        row_max = jnp.max(scores, axis=1, keepdims=True)
        raised = jnp.exp(scores - row_max)
        inverse = 1.0 / jnp.sum(raised, axis=1, keepdims=True)
        exact = raised * inverse
        mean = jnp.sum(exact * tangent, axis=1, keepdims=True)
        weights = exact.astype(jnp.bfloat16)
        turned = (exact * (tangent - mean)).astype(jnp.bfloat16)
        plain = lax.dot_general(weights, values, NN, preferred_element_type=jnp.float32)
        moved = lax.dot_general(turned, values[:, :HEAD], NN, preferred_element_type=jnp.float32)
        result[h, where, :HEAD] = plain[:, :HEAD].astype(jnp.bfloat16)
        result[h, where, HEAD:] = (moved + plain[:, HEAD:]).astype(jnp.bfloat16)

        @pl.when((g > 0) & (lax.rem(g + steps - 1, steps) < kept))
        def _():
            give_block(g - 1)

        return carry

    lax.fori_loop(0, per_group * steps, block, 0)
    sent = held.at[:, :, pl.ds(0, (groups - 1) * rows), :]
    pltpu.make_async_copy(sent, sent, in_send).wait()
    for i in range(kept, steps):
        for h in range(per_group):
            give_block(h * steps + i)
    given = result.at[:, pl.ds(0, (groups - 1) * rows), :]
    pltpu.make_async_copy(given, given, out_send).wait()
    pltpu.make_async_copy(out_ref, out_ref, out_recv.at[0]).wait()
    pltpu.make_async_copy(dout_ref, dout_ref, out_recv.at[1]).wait()


def put_out(a_ref, b_ref, a_out, b_out, sems):
    copies = [
        pltpu.make_async_copy(a_ref, a_out, sems.at[0]),
        pltpu.make_async_copy(b_ref, b_out, sems.at[1]),
    ]
    for copy in copies:
        copy.start()
    for copy in copies:
        copy.wait()


def on_device(*args):
    groups = lax.axis_size("seq")
    per_group = HEADS // groups
    tokens = args[0].shape[0] * groups
    shape = jax.ShapeDtypeStruct(args[0].shape, jnp.bfloat16)
    landed = pl.pallas_call(
        functools.partial(kernel, groups),
        out_shape=(pltpu.VMEM(args[0].shape, jnp.bfloat16),) * 2,
        in_specs=[pl.BlockSpec(memory_space=pl.ANY)] * 6,
        out_specs=(pl.BlockSpec(memory_space=pl.ANY),) * 2,
        scratch_shapes=[
            pltpu.VMEM((per_group, 3, tokens, 2 * HEAD), jnp.bfloat16),
            pltpu.VMEM((per_group, tokens, 2 * HEAD), jnp.bfloat16),
            pltpu.SemaphoreType.DMA,
            pltpu.SemaphoreType.DMA((per_group,)),
            pltpu.SemaphoreType.DMA,
            pltpu.SemaphoreType.DMA((2,)),
            pltpu.SemaphoreType.REGULAR((groups // 4,)),
        ],
        compiler_params=pltpu.CompilerParams(collective_id=0, has_side_effects=True),
        name="attention_tangent",
    )(*args)
    return pl.pallas_call(
        put_out,
        out_shape=(shape, shape),
        in_specs=[pl.BlockSpec(memory_space=pl.ANY)] * 2,
        out_specs=(pl.BlockSpec(memory_space=pl.ANY),) * 2,
        scratch_shapes=[pltpu.SemaphoreType.DMA((2,))],
        name="put_out",
    )(*(pltpu.with_memory_space_constraint(x, pltpu.VMEM) for x in landed))


def solution(mesh):
    spec = P(("dp", "seq"), None)
    return jax.shard_map(
        on_device, mesh=mesh, in_specs=(spec,) * 6, out_specs=(spec, spec), check_vma=False
    )
```

```python
import functools

import jax
import jax.numpy as jnp
from jax import lax
from jax.experimental import pallas as pl
from jax.experimental.pallas import tpu as pltpu
from jax.sharding import PartitionSpec as P

HEADS = 32
HEAD = 128
MESH_ID = pl.DeviceIdType.MESH
NT = (((1,), (1,)), ((), ()))
NN = (((1,), (0,)), ((), ()))


def kernel(
    groups,
    q_ref,
    k_ref,
    v_ref,
    dq_ref,
    dk_ref,
    dv_ref,
    out_ref,
    dout_ref,
    held,
    result,
    in_send,
    in_recv,
    out_send,
    out_recv,
    rounds,
):
    me = lax.axis_index("seq")
    rows = q_ref.shape[0]
    per_group = HEADS // groups
    steps = groups // 2
    pair = 2 * rows
    scale = HEAD ** (-0.5)
    my_z, my_y = me // 2, me % 2

    def far_first(i):
        distance = (steps - i) // 2
        sign = 2 * (i % 2) - 1
        return lax.rem(my_z + sign * distance + steps, steps)

    def at(distance, y):
        return lax.rem(my_z + distance + steps, steps) * 2 + y

    neighbours = (at(1, my_y), at(-1, my_y))
    barrier = pltpu.get_barrier_semaphore()
    for peer in neighbours + (at(0, 1 - my_y),):
        pl.semaphore_signal(barrier, inc=1, device_id={"seq": peer}, device_id_type=MESH_ID)

    plan = ((k_ref, 1, 0), (dk_ref, 1, HEAD), (dq_ref, 0, 0), (q_ref, 0, HEAD), (v_ref, 2, 0), (dv_ref, 2, HEAD))

    def piece(source, kind, column, h, peer):
        src = source.at[:, pl.ds(pl.multiple_of((peer * per_group + h) * HEAD, HEAD), HEAD)]
        dst = held.at[h, kind, pl.ds(pl.multiple_of(me * rows, rows), rows), pl.ds(column, HEAD)]
        return src, dst

    for h in range(per_group):
        for source, kind, column in plan:
            src, dst = piece(source, kind, column, h, me)
            pltpu.make_async_copy(src, dst, in_recv.at[h]).start()

    def send_to(h, peer, part=plan):
        for source, kind, column in part:
            src, dst = piece(source, kind, column, h, peer)
            pltpu.make_async_remote_copy(
                src_ref=src,
                dst_ref=dst,
                send_sem=in_send,
                recv_sem=in_recv.at[h],
                device_id={"seq": peer},
                device_id_type=MESH_ID,
            ).start()

    pl.semaphore_wait(barrier, 3)
    half = steps // 2
    for hops in range(1, half + 2):
        if hops > 1:
            for peer in neighbours:
                pl.semaphore_signal(
                    rounds.at[hops - 2], inc=1, device_id={"seq": peer}, device_id_type=MESH_ID
                )
            pl.semaphore_wait(rounds.at[hops - 2], 2)
        for distance, y in ((hops - 1, 1 - my_y), (hops, my_y)):
            if distance <= half:
                for sign in (1, -1) if 0 < distance < half else (1,):
                    send_to(0, at(sign * distance, y))

    for h in range(1, per_group):
        for entry in plan:

            def send_rest(j, carry, h=h, entry=entry):
                peer = far_first(lax.rem(j, steps)) * 2 + lax.rem(my_y + 1 + j // steps, 2)
                send_to(h, peer, (entry,))
                return carry

            lax.fori_loop(0, groups - 1, send_rest, 0)

    def give(g, target_y, own):
        h, z = g // steps, far_first(g % steps)
        target = z * 2 + target_y
        for part, ref in ((0, out_ref), (1, dout_ref)):
            src = result.at[h, pl.ds(pl.multiple_of(target * rows, rows), rows), pl.ds(part * HEAD, HEAD)]
            dst = ref.at[:, pl.ds(pl.multiple_of((me * per_group + h) * HEAD, HEAD), HEAD)]
            if own:
                pltpu.make_async_copy(src, dst, out_recv.at[part]).start()
            else:
                pltpu.make_async_remote_copy(
                    src_ref=src,
                    dst_ref=dst,
                    send_sem=out_send,
                    recv_sem=out_recv.at[part],
                    device_id={"seq": target},
                    device_id_type=MESH_ID,
                ).start()

    def give_block(g):
        give(g, 1 - my_y, False)

        @pl.when(g % steps == steps - 1)
        def _():
            give(g, my_y, True)

        @pl.when(g % steps != steps - 1)
        def _():
            give(g, my_y, False)

    kept = steps - 3

    def block(g, carry):
        h = g // steps

        @pl.when(g % steps == 0)
        def _():
            pltpu.make_async_copy(held.at[h], held.at[h], in_recv.at[h]).wait()

        where = pl.ds(pl.multiple_of(far_first(g % steps) * pair, pair), pair)
        both = held[h, 0, where, :]
        keys = held[h, 1]
        values = held[h, 2]
        scores = scale * lax.dot_general(
            both[:, HEAD:], keys[:, :HEAD], NT, preferred_element_type=jnp.float32
        )
        tangent = scale * lax.dot_general(both, keys, NT, preferred_element_type=jnp.float32)
        row_max = jnp.max(scores, axis=1, keepdims=True)
        raised = jnp.exp(scores - row_max)
        inverse = 1.0 / jnp.sum(raised, axis=1, keepdims=True)
        exact = raised * inverse
        mean = jnp.sum(exact * tangent, axis=1, keepdims=True)
        weights = exact.astype(jnp.bfloat16)
        turned = (exact * (tangent - mean)).astype(jnp.bfloat16)
        plain = lax.dot_general(weights, values, NN, preferred_element_type=jnp.float32)
        moved = lax.dot_general(turned, values[:, :HEAD], NN, preferred_element_type=jnp.float32)
        result[h, where, :HEAD] = plain[:, :HEAD].astype(jnp.bfloat16)
        result[h, where, HEAD:] = (moved + plain[:, HEAD:]).astype(jnp.bfloat16)

        @pl.when((g > 0) & (lax.rem(g + steps - 1, steps) < kept))
        def _():
            give_block(g - 1)

        return carry

    lax.fori_loop(0, per_group * steps, block, 0)
    sent = held.at[:, :, pl.ds(0, (groups - 1) * rows), :]
    pltpu.make_async_copy(sent, sent, in_send).wait()
    for i in range(kept, steps):
        for h in range(per_group):
            give_block(h * steps + i)
    given = result.at[:, pl.ds(0, (groups - 1) * rows), :]
    pltpu.make_async_copy(given, given, out_send).wait()
    pltpu.make_async_copy(out_ref, out_ref, out_recv.at[0]).wait()
    pltpu.make_async_copy(dout_ref, dout_ref, out_recv.at[1]).wait()


def put_out(a_ref, b_ref, a_out, b_out, sems):
    copies = [
        pltpu.make_async_copy(a_ref, a_out, sems.at[0]),
        pltpu.make_async_copy(b_ref, b_out, sems.at[1]),
    ]
    for copy in copies:
        copy.start()
    for copy in copies:
        copy.wait()


def on_device(*args):
    groups = lax.axis_size("seq")
    per_group = HEADS // groups
    tokens = args[0].shape[0] * groups
    shape = jax.ShapeDtypeStruct(args[0].shape, jnp.bfloat16)
    landed = pl.pallas_call(
        functools.partial(kernel, groups),
        out_shape=(pltpu.VMEM(args[0].shape, jnp.bfloat16),) * 2,
        in_specs=[pl.BlockSpec(memory_space=pl.ANY)] * 6,
        out_specs=(pl.BlockSpec(memory_space=pl.ANY),) * 2,
        scratch_shapes=[
            pltpu.VMEM((per_group, 3, tokens, 2 * HEAD), jnp.bfloat16),
            pltpu.VMEM((per_group, tokens, 2 * HEAD), jnp.bfloat16),
            pltpu.SemaphoreType.DMA,
            pltpu.SemaphoreType.DMA((per_group,)),
            pltpu.SemaphoreType.DMA,
            pltpu.SemaphoreType.DMA((2,)),
            pltpu.SemaphoreType.REGULAR((groups // 4,)),
        ],
        compiler_params=pltpu.CompilerParams(collective_id=0, has_side_effects=True),
        name="attention_tangent",
    )(*args)
    return pl.pallas_call(
        put_out,
        out_shape=(shape, shape),
        in_specs=[pl.BlockSpec(memory_space=pl.ANY)] * 2,
        out_specs=(pl.BlockSpec(memory_space=pl.ANY),) * 2,
        scratch_shapes=[pltpu.SemaphoreType.DMA((2,))],
        name="put_out",
    )(*(pltpu.with_memory_space_constraint(x, pltpu.VMEM) for x in landed))


def solution(mesh):
    spec = P(("dp", "seq"), None)
    return jax.shard_map(
        on_device, mesh=mesh, in_specs=(spec,) * 6, out_specs=(spec, spec), check_vma=False
    )
```
